512 devices in a mesh: dp: 64 (over z, y), own: 8 (over x, core).
Axes of the slice: x: 4, y: 8, z: 8, core: 2. Of those that a mesh axis runs over, the one named last changes fastest.
Arguments:
- partial_grads: bfloat16 [64, 112, 16, 4096], P('dp', None, 'own'), may hold values from -1 to 1
- owner_group: int32 [112], replicated, may hold values from 0 to 63, as said below
- master: float32 [128, 16, 4096], P('dp', 'own'), may hold values from -12 to 12
- moment_one: float32 [128, 16, 4096], P('dp', 'own'), may hold values from -3 to 3
- moment_two: float32 [128, 16, 4096], P('dp', 'own'), may hold values from 0.01 to 1
- vec_grads: bfloat16 [64, 64, 4096], P('dp', None, 'own'), may hold values from -1 to 1
- vec_master: float32 [64, 4096], P(None, 'own'), may hold values from 0.5 to 1.5
- vec_first: float32 [64, 4096], P(None, 'own'), may hold values from -3 to 3
- vec_second: float32 [64, 4096], P(None, 'own'), may hold values from 0.01 to 1
Outputs:
- new_master: float32 [128, 16, 4096], P('dp', 'own')
- new_first: float32 [128, 16, 4096], P('dp', 'own')
- new_second: float32 [128, 16, 4096], P('dp', 'own')
- weights: bfloat16 [112, 16, 4096], P(None, 'own')
- new_vec_master: float32 [64, 4096], P(None, 'own')
- new_vec_first: float32 [64, 4096], P(None, 'own')
- new_vec_second: float32 [64, 4096], P(None, 'own')
The draws below stay inside these ranges and needn't reach their ends.
Inputs may be any that keep to these rules, and one draw needn't show every extreme that they name: `owner_group`: each owner group is named by at most 2 matrices, and some group by exactly 2.
All inputs are finite; a program needn't handle non-finite values.
Results may differ from the reference program's by a relative error of at most 0.001.
Values may be sent and summed in bfloat16 or wider, within the bound.
No kernel may reach another device: no remote copies, remote signals or barrier semaphores. Data moves between devices by JAX's collectives and lax.ppermute only.
A program may use at most 64 MiB of HBM per device.

```python
import math
import jax
import jax.numpy as jnp
from jax import lax

D = 4096
ROWS = 16
CAP = 2
NMAT = 112
NVEC = 64
N_DP = 64


def draw_owner_group(key, part):
    order = jax.random.permutation(key, N_DP * CAP)
    return (order[:NMAT] // CAP).astype(jnp.int32)


def draw_master(key, part):
    key_base = jax.random.fold_in(key, 11)
    key_rows = jax.random.fold_in(key, 12)
    key_cols = jax.random.fold_in(key, 13)
    shape = (N_DP * CAP, ROWS, D)
    base = jnp.clip(jax.random.normal(key_base, shape, jnp.float32), -4.0, 4.0)
    spread = math.log(10.0)
    rising = jnp.arange(ROWS, dtype=jnp.float32)[None, :, None] / (ROWS - 1.0)
    row_part = math.log(3.0) * (rising - 1.0) + spread * (jax.random.uniform(key_rows, (N_DP * CAP, ROWS, 1), jnp.float32) - 1.0)
    col_part = spread * (jax.random.uniform(key_cols, (N_DP * CAP, 1, D), jnp.float32) - 1.0)
    return (3.0 * base * jnp.exp(row_part + col_part)).astype(jnp.float32)


def with_spikes(result, stream_key, source, target, parts, factor):
    def block_of(axis_at):
        return (jnp.arange(result.shape[axis_at]) // (result.shape[axis_at] // parts)).reshape((-1,) + (1,) * (result.ndim - 1 - axis_at))

    near = jax.random.permutation(stream_key, parts)[block_of(target)]
    far = (block_of(target) + parts // 2) % parts
    return jnp.where((block_of(source) == near) | (block_of(source) == far), factor * result, result)


def level_of(stream_key, shape, shards, smallest, largest):
    level = 1.0
    for dim, shards_of in shards:
        heights = jax.random.uniform(jax.random.fold_in(jax.random.fold_in(stream_key, 6), dim), (shards_of,), jnp.float32, smallest / len(shards), largest / len(shards))
        level = level * jnp.repeat(jnp.exp(heights), shape[dim] // shards_of).reshape((-1,) + (1,) * (len(shape) - 1 - dim))
    return level


def scatter_about(rng, dims, scale, limit, cuts=(), kind=jnp.bfloat16):
    values = jax.random.normal(rng, dims, jnp.float32) * scale
    if len(cuts) > 0:
        values = level_of(rng, dims, cuts, -0.22, 0.18) * values
    return jnp.clip(values, min=-limit, max=limit).astype(kind)


def noise_with(own_key, dims, scale, reach, cuts, heavy, kind=jnp.bfloat16):
    array = scale * jax.random.normal(own_key, dims, jnp.float32)
    if cuts:
        array = array * level_of(own_key, dims, cuts, -0.22, 0.18)
    return jnp.clip(with_spikes(array, jax.random.fold_in(own_key, 3), *heavy), -reach, reach).astype(kind)


def setup_inputs(seed: int = 0) -> dict:
    arg_keys = jax.random.split(jax.random.key(seed), 10)
    partial_grads = noise_with(arg_keys[0], (N_DP, NMAT, ROWS, D), 0.125, 1.0, ((0, 64), (2, 8)), (0, 1, 16, 2.0))
    owner_group = draw_owner_group(jax.random.fold_in(arg_keys[9], 71), 0)
    master = draw_master(jax.random.fold_in(arg_keys[9], 71), 0)
    moment_one = scatter_about(arg_keys[3], (N_DP * CAP, ROWS, D), 0.5, 3.0, ((0, 64), (1, 8)), jnp.float32)
    moment_two = jnp.clip(jnp.exp(math.log(1.0) - 4.6051702 * jax.random.uniform(arg_keys[4], (N_DP * CAP, ROWS, D), jnp.float32) ** level_of(arg_keys[4], (N_DP * CAP, ROWS, D), ((0, 64), (1, 8)), -0.2, 0.2)), 0.01, 1.0)
    vec_grads = scatter_about(arg_keys[5], (N_DP, NVEC, D), 0.125, 1.0, ((0, 64), (2, 8)))
    vec_master = jnp.clip(1.0 + 0.1 * jax.random.normal(arg_keys[6], (NVEC, D), jnp.float32), 0.5, 1.5)
    vec_first = scatter_about(arg_keys[7], (NVEC, D), 0.5, 3.0, ((1, 8),), jnp.float32)
    vec_second = jnp.clip(jnp.exp(math.log(1.0) - 4.6051702 * jax.random.uniform(arg_keys[8], (NVEC, D), jnp.float32) ** level_of(arg_keys[8], (NVEC, D), ((1, 8),), -0.2, 0.2)), 0.01, 1.0)
    return dict(partial_grads=partial_grads, owner_group=owner_group, master=master, moment_one=moment_one, moment_two=moment_two, vec_grads=vec_grads, vec_master=vec_master, vec_first=vec_first, vec_second=vec_second)


beta_one = 0.9
beta_two = 0.95
fix_one = 1.0 - 0.9 ** 10
fix_two = 1.0 - 0.95 ** 10
epsilon = 1e-06
decay_rate = 0.1
learn_rate = 0.05

def slot_numbers(owner_group, capacity):
    count = owner_group.shape[0]
    places = jnp.arange(count, dtype=jnp.int32)
    same = owner_group[:, None] == owner_group[None, :]
    before = places[None, :] < places[:, None]
    ranks = lax.optimization_barrier(jnp.sum((same & before).astype(jnp.int32), axis=1)).astype(jnp.int32)
    return (owner_group * capacity + ranks).astype(jnp.int32)

def reference(partial_grads, owner_group, master, moment_one, moment_two, vec_grads, vec_master, vec_first, vec_second):

    def accumulate(index, total):
        return total + partial_grads[index].astype(jnp.float32)
    summed = lax.fori_loop(0, N_DP, accumulate, jnp.zeros((NMAT, ROWS, D), jnp.float32))
    slots = slot_numbers(owner_group, CAP)
    gradient = jnp.zeros((N_DP * CAP, ROWS, D), jnp.float32).at[slots].set(summed)
    filled = jnp.zeros((N_DP * CAP,), jnp.float32).at[slots].set(1.0)[:, None, None]
    first_raw = beta_one * moment_one + (1.0 - beta_one) * gradient
    second_raw = beta_two * moment_two + (1.0 - beta_two) * gradient * gradient
    update = first_raw / fix_one / (jnp.sqrt(second_raw / fix_two) + epsilon) + decay_rate * master
    weight_sq = lax.optimization_barrier(jnp.sum(master * master, axis=(1, 2)))
    update_sq = lax.optimization_barrier(jnp.sum(update * update, axis=(1, 2)))
    ratio = jnp.sqrt(weight_sq) / jnp.sqrt(update_sq)
    new_master = filled * (master - learn_rate * ratio[:, None, None] * update)
    new_first = filled * first_raw
    new_second = filled * second_raw
    weights = new_master[slots].astype(jnp.bfloat16)
    vec_gradient = lax.optimization_barrier(jnp.sum(vec_grads.astype(jnp.float32), axis=0))
    new_vec_first = beta_one * vec_first + (1.0 - beta_one) * vec_gradient
    new_vec_second = beta_two * vec_second + (1.0 - beta_two) * vec_gradient * vec_gradient
    new_vec_master = vec_master - learn_rate * (new_vec_first / fix_one) / (jnp.sqrt(new_vec_second / fix_two) + epsilon)
    return (new_master, new_first, new_second, weights, new_vec_master, new_vec_first, new_vec_second)
```

```python
import functools

import jax
import jax.numpy as jnp
from jax import lax
from jax.experimental import pallas as pl
from jax.experimental.pallas import tpu as pltpu
from jax.sharding import PartitionSpec as P

beta_one = 0.9
beta_two = 0.95
fix_one = 1.0 - 0.9**10
fix_two = 1.0 - 0.95**10
epsilon = 1e-06
decay_rate = 0.1
learn_rate = 0.05

SIDE = 8
CAP = 2
LANES = 128
ROWS = 64
SLOT_ROWS = CAP * ROWS
VEC_ROWS = 4
PART = SIDE * SLOT_ROWS
WIDE = PART + SIDE * VEC_ROWS
CHUNK = SLOT_ROWS + 2 * VEC_ROWS

VMEM = pl.BlockSpec(memory_space=pltpu.VMEM)
SMEM = pl.BlockSpec(memory_space=pltpu.SMEM)
ANY = pl.BlockSpec(memory_space=pl.ANY)


def place_of(group):
    core = lax.rem(lax.axis_index("own"), 2)
    z, y = group // SIDE, lax.rem(group, SIDE)
    return jnp.where(core == 0, y, z), jnp.where(core == 0, z, y)


def pack_kernel(owner, grads, vecs, out, held, sem, vec_sem):
    count = owner.shape[0]

    def clear(g, _):
        held[g] = 0
        return 0

    lax.fori_loop(0, SIDE * SIDE, clear, 0, unroll=8)
    vec_copy = pltpu.make_async_copy(vecs, out.at[:, pl.ds(PART, SIDE * VEC_ROWS), :], vec_sem)
    vec_copy.start()

    def send(m, _):
        g = owner[m]
        rank = held[g]
        held[g] = rank + 1
        far, near = place_of(g)
        row = pl.multiple_of(near * SLOT_ROWS + rank * ROWS, ROWS)
        pltpu.make_async_copy(grads.at[m], out.at[far, pl.ds(row, ROWS), :], sem).start()
        return 0

    lax.fori_loop(0, count, send, 0, unroll=4)

    def empty(g, _):
        far, near = place_of(g)
        for rank in range(CAP):

            @pl.when(held[g] <= rank)
            def _():
                row = pl.multiple_of(near * SLOT_ROWS + rank * ROWS, ROWS)
                out[far, pl.ds(row, ROWS), :] = jnp.zeros((ROWS, LANES), out.dtype)

        return 0

    lax.fori_loop(0, SIDE * SIDE, empty, 0, unroll=2)
    vec_copy.wait()
    pltpu.make_async_copy(grads, grads, sem).wait()


def partial_sum_kernel(got, out):
    for near in range(SIDE):
        rows = pl.ds(near * SLOT_ROWS, SLOT_ROWS)
        total = got[0, rows, :].astype(jnp.float32)
        for far in range(1, SIDE):
            total = total + got[far, rows, :].astype(jnp.float32)
        out[near, pl.ds(0, SLOT_ROWS), :] = total
    total = got[0, pl.ds(PART, SIDE * VEC_ROWS), :].astype(jnp.float32)
    for far in range(1, SIDE):
        total = total + got[far, pl.ds(PART, SIDE * VEC_ROWS), :].astype(jnp.float32)
    for near in range(SIDE):
        out[near, pl.ds(SLOT_ROWS, VEC_ROWS), :] = total[near * VEC_ROWS : (near + 1) * VEC_ROWS]
        out[near, pl.ds(SLOT_ROWS + VEC_ROWS, VEC_ROWS), :] = jnp.zeros((VEC_ROWS, LANES), jnp.float32)


def update_kernel(held, got, master, one, two, new_first, new_second, update_out, norms, vec_out):
    mine = held[lax.axis_index("dp")]
    for slot in range(CAP):
        rows = pl.ds(slot * ROWS, ROWS)
        gradient = got[0, rows, :]
        for k in range(1, SIDE):
            gradient = gradient + got[k, rows, :]
        weight = master[rows, :]
        first = beta_one * one[rows, :] + (1.0 - beta_one) * gradient
        second = beta_two * two[rows, :] + (1.0 - beta_two) * gradient * gradient
        update = first / fix_one / (jnp.sqrt(second / fix_two) + epsilon) + decay_rate * weight
        keep = mine > slot
        new_first[rows, :] = jnp.where(keep, first, 0.0)
        new_second[rows, :] = jnp.where(keep, second, 0.0)
        update_out[rows, :] = update
        weight_sq = jnp.sum((weight * weight).reshape(ROWS // 8, 8, LANES), axis=0)
        update_sq = jnp.sum((update * update).reshape(ROWS // 8, 8, LANES), axis=0)
        for k in range(SIDE):
            norms[k, pl.ds(2 * slot, 1), :] = jnp.sum(weight_sq, axis=0, keepdims=True)
            norms[k, pl.ds(2 * slot + 1, 1), :] = jnp.sum(update_sq, axis=0, keepdims=True)
    for k in range(SIDE):
        norms[k, pl.ds(2 * CAP, 8 - 2 * CAP), :] = jnp.zeros((8 - 2 * CAP, LANES), jnp.float32)
    rows = pl.ds(SLOT_ROWS, VEC_ROWS)
    total = got[0, rows, :]
    for k in range(1, SIDE):
        total = total + got[k, rows, :]
    vec_out[pl.ds(0, VEC_ROWS), :] = total
    vec_out[pl.ds(VEC_ROWS, VEC_ROWS), :] = total - total.astype(jnp.bfloat16).astype(jnp.float32)


def step_kernel(held, norms, master, update, vec, new_master, out):
    mine = held[lax.axis_index("dp")]
    total = norms[0]
    for k in range(1, SIDE):
        total = total + norms[k]
    total = jnp.sum(total, axis=1, keepdims=True)
    for slot in range(CAP):
        rows = pl.ds(slot * ROWS, ROWS)
        ratio = jnp.sqrt(total[2 * slot : 2 * slot + 1]) / jnp.sqrt(total[2 * slot + 1 : 2 * slot + 2])
        stepped = master[rows, :] - learn_rate * ratio * update[rows, :]
        stepped = jnp.where(mine > slot, stepped, 0.0)
        new_master[rows, :] = stepped
        rounded = stepped.astype(jnp.bfloat16)
        for k in range(SIDE):
            out[k, rows, :] = rounded
    rounded = vec[...].astype(jnp.bfloat16)
    for k in range(SIDE):
        out[k, pl.ds(SLOT_ROWS, 2 * VEC_ROWS), :] = rounded


def repeat_kernel(got, out):
    for near in range(SIDE):
        block = got[near]
        for k in range(SIDE):
            out[k, pl.ds(near * CHUNK, CHUNK), :] = block


def unpack_kernel(owner, got, vec_master, vec_first, vec_second, weights, new_master, new_first, new_second, held, sem):
    count = owner.shape[0]

    def clear(g, _):
        held[g] = 0
        return 0

    lax.fori_loop(0, SIDE * SIDE, clear, 0, unroll=8)

    def fetch(m, _):
        g = owner[m]
        rank = held[g]
        held[g] = rank + 1
        far, near = place_of(g)
        row = pl.multiple_of(near * CHUNK + rank * ROWS, 8)
        pltpu.make_async_copy(got.at[far, pl.ds(row, ROWS), :], weights.at[m], sem).start()
        return 0

    lax.fori_loop(0, count, fetch, 0, unroll=4)
    for far in range(SIDE):
        pieces = []
        for near in range(SIDE):
            both = got[far, pl.ds(near * CHUNK + SLOT_ROWS, 2 * VEC_ROWS), :].astype(jnp.float32)
            pieces.append(both[:VEC_ROWS] + both[VEC_ROWS:])
        gradient = jnp.concatenate(pieces, axis=0)
        first = beta_one * vec_first[far] + (1.0 - beta_one) * gradient
        second = beta_two * vec_second[far] + (1.0 - beta_two) * gradient * gradient
        new_first[far] = first
        new_second[far] = second
        new_master[far] = vec_master[far] - learn_rate * (first / fix_one) / (jnp.sqrt(second / fix_two) + epsilon)
    pltpu.make_async_copy(weights, weights, sem).wait()


def to_rows(block):
    n, r, columns = block.shape
    return block.reshape(n, r, columns // LANES, LANES).transpose(0, 2, 1, 3).reshape(n, ROWS, LANES)


def from_rows(rows):
    n = rows.shape[0]
    return rows.reshape(n, ROWS // 2, 2, LANES).transpose(0, 2, 1, 3).reshape(n, 2, ROWS // 2 * LANES)


def vec_rows(block):
    return block.reshape(SIDE, SIDE, 4, LANES).transpose(0, 2, 1, 3).reshape(SIDE, 4 * SIDE, LANES)


def from_vec_rows(rows):
    return rows.reshape(SIDE, 4, SIDE, LANES).transpose(0, 2, 1, 3).reshape(SIDE * SIDE, 4 * LANES)


def axis_groups():
    def device(z, y, x, core):
        return (z * SIDE + y) * 8 + x * 2 + core

    side = range(SIDE)

    def along_y(core):
        return [[device(z, y, x, core) for y in side] for z in side for x in range(4)]

    def along_z(core):
        return [[device(z, y, x, core) for z in side] for y in side for x in range(4)]

    return along_y(0) + along_z(1), along_z(0) + along_y(1)


def exchange(x, groups):
    return lax.all_to_all(x, ("dp", "own"), 0, 0, axis_index_groups=groups, tiled=True)


def vmem(shape, dtype):
    return pltpu.VMEM(shape, dtype)


def body(
    partial_grads,
    owner_group,
    master,
    moment_one,
    moment_two,
    vec_grads,
    vec_master,
    vec_first,
    vec_second,
):
    f32, bf16 = jnp.float32, jnp.bfloat16
    first_groups, second_groups = axis_groups()
    count = owner_group.shape[0]
    packed, held = pl.pallas_call(
        pack_kernel,
        out_shape=(jax.ShapeDtypeStruct((SIDE, WIDE, LANES), bf16), jax.ShapeDtypeStruct((SIDE * SIDE,), jnp.int32)),
        in_specs=[SMEM, ANY, ANY],
        out_specs=(VMEM, SMEM),
        scratch_shapes=[pltpu.SemaphoreType.DMA, pltpu.SemaphoreType.DMA],
        name="pack",
    )(owner_group, to_rows(partial_grads[0]), vec_rows(vec_grads[0]))
    got = exchange(packed, first_groups)
    partial = pl.pallas_call(
        partial_sum_kernel,
        out_shape=jax.ShapeDtypeStruct((SIDE, CHUNK, LANES), f32),
        in_specs=[VMEM],
        out_specs=VMEM,
        name="partial_sum",
    )(got)
    got = exchange(partial, second_groups)
    block = jax.ShapeDtypeStruct((SLOT_ROWS, LANES), f32)
    master_rows = to_rows(master).reshape(SLOT_ROWS, LANES)
    new_first, new_second, update, norms, vec_sum = pl.pallas_call(
        update_kernel,
        out_shape=(
            block,
            block,
            block,
            jax.ShapeDtypeStruct((SIDE, 8, LANES), f32),
            jax.ShapeDtypeStruct((2 * VEC_ROWS, LANES), f32),
        ),
        in_specs=[SMEM] + [VMEM] * 4,
        out_specs=(VMEM,) * 5,
        name="update",
    )(
        held,
        got,
        master_rows,
        to_rows(moment_one).reshape(SLOT_ROWS, LANES),
        to_rows(moment_two).reshape(SLOT_ROWS, LANES),
    )
    norms = lax.all_to_all(norms, "own", 0, 0, tiled=True)
    new_master, out = pl.pallas_call(
        step_kernel,
        out_shape=(block, jax.ShapeDtypeStruct((SIDE, CHUNK, LANES), bf16)),
        in_specs=[SMEM] + [VMEM] * 4,
        out_specs=(VMEM, VMEM),
        name="step",
    )(held, norms, master_rows, update, vec_sum)
    got = exchange(out, second_groups)
    out = pl.pallas_call(
        repeat_kernel,
        out_shape=jax.ShapeDtypeStruct((SIDE, SIDE * CHUNK, LANES), bf16),
        in_specs=[VMEM],
        out_specs=VMEM,
        name="repeat",
    )(got)
    got = exchange(out, first_groups)
    vec_block = jax.ShapeDtypeStruct((SIDE, 4 * SIDE, LANES), f32)
    weights, new_vec_master, new_vec_first, new_vec_second = pl.pallas_call(
        unpack_kernel,
        out_shape=(jax.ShapeDtypeStruct((count, ROWS, LANES), bf16), vec_block, vec_block, vec_block),
        in_specs=[SMEM, VMEM, VMEM, VMEM, VMEM],
        out_specs=(ANY, VMEM, VMEM, VMEM),
        scratch_shapes=[pltpu.SMEM((SIDE * SIDE,), jnp.int32), pltpu.SemaphoreType.DMA],
        name="unpack",
    )(owner_group, got, vec_rows(vec_master), vec_rows(vec_first), vec_rows(vec_second))

    def slots(rows):
        return from_rows(rows.reshape(CAP, ROWS, LANES))

    return (
        slots(new_master),
        slots(new_first),
        slots(new_second),
        from_rows(weights),
        from_vec_rows(new_vec_master),
        from_vec_rows(new_vec_first),
        from_vec_rows(new_vec_second),
    )


def solution(mesh):
    placed = (
        P("dp", None, "own", None),
        P(),
        P("dp", "own", None),
        P("dp", "own", None),
        P("dp", "own", None),
        P("dp", None, "own"),
        P(None, "own"),
        P(None, "own"),
        P(None, "own"),
    )
    return jax.shard_map(
        body,
        mesh=mesh,
        in_specs=placed,
        out_specs=(
            P("dp", "own", None),
            P("dp", "own", None),
            P("dp", "own", None),
            P(None, "own", None),
            P(None, "own"),
            P(None, "own"),
            P(None, "own"),
        ),
        check_vma=False,
    )
```

```python
import functools

import jax
import jax.numpy as jnp
from jax import lax
from jax.experimental import pallas as pl
from jax.experimental.pallas import tpu as pltpu
from jax.sharding import PartitionSpec as P

beta_one = 0.9
beta_two = 0.95
fix_one = 1.0 - 0.9**10
fix_two = 1.0 - 0.95**10
epsilon = 1e-06
decay_rate = 0.1
learn_rate = 0.05

SIDE = 8
CAP = 2
LANES = 128
ROWS = 64
SLOT_ROWS = CAP * ROWS
VEC_ROWS = 4
PART = SIDE * SLOT_ROWS
WIDE = PART + SIDE * VEC_ROWS
CHUNK = SLOT_ROWS + 2 * VEC_ROWS

VMEM = pl.BlockSpec(memory_space=pltpu.VMEM)
SMEM = pl.BlockSpec(memory_space=pltpu.SMEM)
ANY = pl.BlockSpec(memory_space=pl.ANY)


def strides(far, near):
    core = lax.rem(lax.axis_index("own"), 2)
    return jnp.where(core == 0, near, far), jnp.where(core == 0, far, near)


def row_of(slot, by_z, by_y, tile):
    z = lax.shift_right_logical(slot, 4)
    y = lax.shift_right_logical(slot, 1) & (SIDE - 1)
    return pl.multiple_of(z * by_z + y * by_y + (slot & 1) * ROWS, tile)


def pack_kernel(owner, grads, vecs, out, slots, held, blank, sem):
    count = owner.shape[0]
    by_z, by_y = strides(WIDE, SLOT_ROWS)
    for far in range(SIDE):
        pltpu.make_async_copy(vecs.at[far], out.at[pl.ds(far * WIDE + PART, SIDE * VEC_ROWS), :], sem).start()
    blank[...] = jnp.zeros_like(blank)

    def clear(g, _):
        held[g] = 0
        return 0

    lax.fori_loop(0, SIDE * SIDE, clear, 0, unroll=16)

    def send(m, _):
        g = owner[m]
        rank = held[g]
        held[g] = rank + 1
        slot = g * CAP + rank
        slots[m] = slot
        row = row_of(slot, by_z, by_y, 32)
        pltpu.make_async_copy(grads.at[m], out.at[pl.ds(row, ROWS), :], sem).start()
        return 0

    lax.fori_loop(0, count, send, 0, unroll=8)

    def empty(g, _):
        filled = held[g]

        @pl.when(filled < CAP)
        def _():
            def put(slot):
                row = row_of(slot, by_z, by_y, 32)
                pltpu.make_async_copy(blank, out.at[pl.ds(row, ROWS), :], sem).start()

            put(g * CAP + 1)

            @pl.when(filled == 0)
            def _():
                put(g * CAP)

        return 0

    lax.fori_loop(0, SIDE * SIDE, empty, 0, unroll=4)
    pltpu.make_async_copy(out, out, sem).wait()


def partial_sum_kernel(got, out):
    for near in range(SIDE):
        rows = pl.ds(near * SLOT_ROWS, SLOT_ROWS)
        total = got[0, rows, :].astype(jnp.float32)
        for far in range(1, SIDE):
            total = total + got[far, rows, :].astype(jnp.float32)
        out[near, pl.ds(0, SLOT_ROWS), :] = total
    total = got[0, pl.ds(PART, SIDE * VEC_ROWS), :].astype(jnp.float32)
    for far in range(1, SIDE):
        total = total + got[far, pl.ds(PART, SIDE * VEC_ROWS), :].astype(jnp.float32)
    for near in range(SIDE):
        out[near, pl.ds(SLOT_ROWS, VEC_ROWS), :] = total[near * VEC_ROWS : (near + 1) * VEC_ROWS]
        out[near, pl.ds(SLOT_ROWS + VEC_ROWS, VEC_ROWS), :] = jnp.zeros((VEC_ROWS, LANES), jnp.float32)


def update_kernel(held, got, master, one, two, new_first, new_second, update_out, norms, vec_out):
    mine = held[lax.axis_index("dp")]
    for slot in range(CAP):
        rows = pl.ds(slot * ROWS, ROWS)
        gradient = got[0, rows, :]
        for k in range(1, SIDE):
            gradient = gradient + got[k, rows, :]
        weight = master[rows, :]
        first = beta_one * one[rows, :] + (1.0 - beta_one) * gradient
        second = beta_two * two[rows, :] + (1.0 - beta_two) * gradient * gradient
        update = first / fix_one / (jnp.sqrt(second / fix_two) + epsilon) + decay_rate * weight
        keep = mine > slot
        new_first[rows, :] = jnp.where(keep, first, 0.0)
        new_second[rows, :] = jnp.where(keep, second, 0.0)
        update_out[rows, :] = update
        weight_sq = jnp.sum((weight * weight).reshape(ROWS // 8, 8, LANES), axis=0)
        update_sq = jnp.sum((update * update).reshape(ROWS // 8, 8, LANES), axis=0)
        for k in range(SIDE):
            norms[k, pl.ds(2 * slot, 1), :] = jnp.sum(weight_sq, axis=0, keepdims=True)
            norms[k, pl.ds(2 * slot + 1, 1), :] = jnp.sum(update_sq, axis=0, keepdims=True)
    for k in range(SIDE):
        norms[k, pl.ds(2 * CAP, 8 - 2 * CAP), :] = jnp.zeros((8 - 2 * CAP, LANES), jnp.float32)
    rows = pl.ds(SLOT_ROWS, VEC_ROWS)
    total = got[0, rows, :]
    for k in range(1, SIDE):
        total = total + got[k, rows, :]
    vec_out[pl.ds(0, VEC_ROWS), :] = total
    vec_out[pl.ds(VEC_ROWS, VEC_ROWS), :] = total - total.astype(jnp.bfloat16).astype(jnp.float32)


def step_kernel(held, norms, master, update, vec, new_master, out):
    mine = held[lax.axis_index("dp")]
    total = norms[0]
    for k in range(1, SIDE):
        total = total + norms[k]
    total = jnp.sum(total, axis=1, keepdims=True)
    for slot in range(CAP):
        rows = pl.ds(slot * ROWS, ROWS)
        ratio = jnp.sqrt(total[2 * slot : 2 * slot + 1]) / jnp.sqrt(total[2 * slot + 1 : 2 * slot + 2])
        stepped = master[rows, :] - learn_rate * ratio * update[rows, :]
        stepped = jnp.where(mine > slot, stepped, 0.0)
        new_master[rows, :] = stepped
        rounded = stepped.astype(jnp.bfloat16)
        for k in range(SIDE):
            out[k, rows, :] = rounded
    rounded = vec[...].astype(jnp.bfloat16)
    for k in range(SIDE):
        out[k, pl.ds(SLOT_ROWS, 2 * VEC_ROWS), :] = rounded


def repeat_kernel(got, out):
    for near in range(SIDE):
        block = got[near]
        for k in range(SIDE):
            out[k, pl.ds(near * CHUNK, CHUNK), :] = block


def unpack_kernel(slots, got, vec_master, vec_first, vec_second, weights, new_master, new_first, new_second, parts, sem, part_sem):
    count = slots.shape[0]
    by_z, by_y = strides(SIDE * CHUNK, CHUNK)
    for k in range(SIDE * SIDE):
        pltpu.make_async_copy(got.at[pl.ds(k * CHUNK + SLOT_ROWS, 2 * VEC_ROWS), :], parts.at[k], part_sem).start()

    def fetch(m, _):
        row = row_of(slots[m], by_z, by_y, 8)
        pltpu.make_async_copy(got.at[pl.ds(row, ROWS), :], weights.at[m], sem).start()
        return 0

    lax.fori_loop(0, count, fetch, 0, unroll=8)
    pltpu.make_async_copy(parts, parts, part_sem).wait()
    for far in range(SIDE):
        both = parts[pl.ds(far * SIDE, SIDE)].astype(jnp.float32)
        gradient = (both[:, :VEC_ROWS] + both[:, VEC_ROWS:]).reshape(SIDE * VEC_ROWS, LANES)
        first = beta_one * vec_first[far] + (1.0 - beta_one) * gradient
        second = beta_two * vec_second[far] + (1.0 - beta_two) * gradient * gradient
        new_first[far] = first
        new_second[far] = second
        new_master[far] = vec_master[far] - learn_rate * (first / fix_one) / (jnp.sqrt(second / fix_two) + epsilon)
    pltpu.make_async_copy(weights, weights, sem).wait()


def to_rows(block):
    n, r, columns = block.shape
    return block.reshape(n, r, columns // LANES, LANES).transpose(0, 2, 1, 3).reshape(n, ROWS, LANES)


def from_rows(rows):
    n = rows.shape[0]
    return rows.reshape(n, ROWS // 2, 2, LANES).transpose(0, 2, 1, 3).reshape(n, 2, ROWS // 2 * LANES)


def vec_rows(block):
    return block.reshape(SIDE, SIDE, 4, LANES).transpose(0, 2, 1, 3).reshape(SIDE, 4 * SIDE, LANES)


def from_vec_rows(rows):
    return rows.reshape(SIDE, 4, SIDE, LANES).transpose(0, 2, 1, 3).reshape(SIDE * SIDE, 4 * LANES)


def axis_groups():
    def device(z, y, x, core):
        return (z * SIDE + y) * 8 + x * 2 + core

    side = range(SIDE)

    def along_y(core):
        return [[device(z, y, x, core) for y in side] for z in side for x in range(4)]

    def along_z(core):
        return [[device(z, y, x, core) for z in side] for y in side for x in range(4)]

    return along_y(0) + along_z(1), along_z(0) + along_y(1)


def exchange(x, groups):
    return lax.all_to_all(x, ("dp", "own"), 0, 0, axis_index_groups=groups, tiled=True)


def vmem(shape, dtype):
    return pltpu.VMEM(shape, dtype)


def close(x):
    return pltpu.with_memory_space_constraint(x, pltpu.VMEM)


def body(
    partial_grads,
    owner_group,
    master,
    moment_one,
    moment_two,
    vec_grads,
    vec_master,
    vec_first,
    vec_second,
):
    f32, bf16 = jnp.float32, jnp.bfloat16
    first_groups, second_groups = axis_groups()
    count = owner_group.shape[0]
    packed, slots, held = pl.pallas_call(
        pack_kernel,
        out_shape=(
            jax.ShapeDtypeStruct((SIDE * WIDE, LANES), bf16),
            jax.ShapeDtypeStruct((count,), jnp.int32),
            jax.ShapeDtypeStruct((SIDE * SIDE,), jnp.int32),
        ),
        in_specs=[SMEM, ANY, ANY],
        out_specs=(ANY, SMEM, SMEM),
        scratch_shapes=[pltpu.VMEM((ROWS, LANES), bf16), pltpu.SemaphoreType.DMA],
        name="pack",
    )(owner_group, to_rows(partial_grads[0]), vec_rows(vec_grads[0]))
    got = close(exchange(packed.reshape(SIDE, WIDE, LANES), first_groups))
    partial = pl.pallas_call(
        partial_sum_kernel,
        out_shape=vmem((SIDE, CHUNK, LANES), f32),
        in_specs=[VMEM],
        out_specs=VMEM,
        name="partial_sum",
    )(got)
    got = close(exchange(partial, second_groups))
    block = jax.ShapeDtypeStruct((SLOT_ROWS, LANES), f32)
    master_rows = close(to_rows(master).reshape(SLOT_ROWS, LANES))
    new_first, new_second, update, norms, vec_sum = pl.pallas_call(
        update_kernel,
        out_shape=(
            block,
            block,
            vmem((SLOT_ROWS, LANES), f32),
            vmem((SIDE, 8, LANES), f32),
            vmem((2 * VEC_ROWS, LANES), f32),
        ),
        in_specs=[SMEM] + [VMEM] * 4,
        out_specs=(VMEM,) * 5,
        name="update",
    )(
        held,
        got,
        master_rows,
        close(to_rows(moment_one).reshape(SLOT_ROWS, LANES)),
        close(to_rows(moment_two).reshape(SLOT_ROWS, LANES)),
    )
    norms = close(lax.all_to_all(norms, "own", 0, 0, tiled=True))
    new_master, out = pl.pallas_call(
        step_kernel,
        out_shape=(block, vmem((SIDE, CHUNK, LANES), bf16)),
        in_specs=[SMEM] + [VMEM] * 4,
        out_specs=(VMEM, VMEM),
        name="step",
    )(held, norms, master_rows, update, vec_sum)
    got = close(exchange(out, second_groups))
    out = pl.pallas_call(
        repeat_kernel,
        out_shape=vmem((SIDE, SIDE * CHUNK, LANES), bf16),
        in_specs=[VMEM],
        out_specs=VMEM,
        name="repeat",
    )(got)
    got = exchange(out, first_groups).reshape(SIDE * SIDE * CHUNK, LANES)
    vec_block = jax.ShapeDtypeStruct((SIDE, 4 * SIDE, LANES), f32)
    weights, new_vec_master, new_vec_first, new_vec_second = pl.pallas_call(
        unpack_kernel,
        out_shape=(jax.ShapeDtypeStruct((count, ROWS, LANES), bf16), vec_block, vec_block, vec_block),
        in_specs=[SMEM, ANY, VMEM, VMEM, VMEM],
        out_specs=(ANY, VMEM, VMEM, VMEM),
        scratch_shapes=[
            pltpu.VMEM((SIDE * SIDE, 2 * VEC_ROWS, LANES), bf16),
            pltpu.SemaphoreType.DMA,
            pltpu.SemaphoreType.DMA,
        ],
        name="unpack",
    )(slots, got, *(close(vec_rows(x)) for x in (vec_master, vec_first, vec_second)))

    def blocks(rows):
        return from_rows(rows.reshape(CAP, ROWS, LANES))

    return (
        blocks(new_master),
        blocks(new_first),
        blocks(new_second),
        from_rows(weights),
        from_vec_rows(new_vec_master),
        from_vec_rows(new_vec_first),
        from_vec_rows(new_vec_second),
    )


def solution(mesh):
    placed = (
        P("dp", None, "own", None),
        P(),
        P("dp", "own", None),
        P("dp", "own", None),
        P("dp", "own", None),
        P("dp", None, "own"),
        P(None, "own"),
        P(None, "own"),
        P(None, "own"),
    )
    return jax.shard_map(
        body,
        mesh=mesh,
        in_specs=placed,
        out_specs=(
            P("dp", "own", None),
            P("dp", "own", None),
            P("dp", "own", None),
            P(None, "own", None),
            P(None, "own"),
            P(None, "own"),
            P(None, "own"),
        ),
        check_vma=False,
    )
```

```python
import functools

import jax
import jax.numpy as jnp
from jax import lax
from jax.experimental import pallas as pl
from jax.experimental.pallas import tpu as pltpu
from jax.sharding import PartitionSpec as P

beta_one = 0.9
beta_two = 0.95
fix_one = 1.0 - 0.9**10
fix_two = 1.0 - 0.95**10
epsilon = 1e-06
decay_rate = 0.1
learn_rate = 0.05

SIDE = 8
CAP = 2
LANES = 128
ROWS = 64
SLOT_ROWS = CAP * ROWS
VEC_ROWS = 4
PART = SIDE * SLOT_ROWS
WIDE = PART + SIDE * VEC_ROWS
CHUNK = SLOT_ROWS + 2 * VEC_ROWS
BATCHES = 4

VMEM = pl.BlockSpec(memory_space=pltpu.VMEM)
SMEM = pl.BlockSpec(memory_space=pltpu.SMEM)
ANY = pl.BlockSpec(memory_space=pl.ANY)


def strides(far, near):
    core = lax.rem(lax.axis_index("own"), 2)
    return jnp.where(core == 0, near, far), jnp.where(core == 0, far, near)


def row_of(slot, by_z, by_y, tile):
    z = lax.shift_right_logical(slot, 4)
    y = lax.shift_right_logical(slot, 1) & (SIDE - 1)
    return pl.multiple_of(z * by_z + y * by_y + (slot & 1) * ROWS, tile)


def pack_kernel(owner, grads, vecs, out, slots, held, sem):
    count = owner.shape[0]
    by_z, by_y = strides(WIDE, SLOT_ROWS)
    for far in range(SIDE):
        pltpu.make_async_copy(vecs.at[far], out.at[pl.ds(far * WIDE + PART, SIDE * VEC_ROWS), :], sem).start()

    def clear(g, _):
        held[g] = 0
        return 0

    lax.fori_loop(0, SIDE * SIDE, clear, 0, unroll=16)

    def send(m, _):
        g = owner[m]
        rank = held[g]
        held[g] = rank + 1
        slot = g * CAP + rank
        slots[m] = slot
        row = row_of(slot, by_z, by_y, 32)
        pltpu.make_async_copy(grads.at[m], out.at[pl.ds(row, ROWS), :], sem).start()
        return 0

    lax.fori_loop(0, count, send, 0, unroll=8)

    def empty(g, _):
        filled = held[g]

        @pl.when(filled < CAP)
        def _():
            def put(slot):
                row = row_of(slot, by_z, by_y, 32)
                out[pl.ds(row, ROWS), :] = jnp.zeros((ROWS, LANES), out.dtype)

            put(g * CAP + 1)

            @pl.when(filled == 0)
            def _():
                put(g * CAP)

        return 0

    lax.fori_loop(0, SIDE * SIDE, empty, 0, unroll=4)
    filled_rows = out.at[pl.ds(0, count * ROWS + SIDE * SIDE * VEC_ROWS), :]
    pltpu.make_async_copy(filled_rows, filled_rows, sem).wait()


def partial_sum_kernel(source, out, got, sems):
    def piece(k):
        rows = pl.ds(k * SLOT_ROWS, SLOT_ROWS if k < SIDE else SIDE * VEC_ROWS)
        return pltpu.make_async_copy(source.at[:, rows, :], got.at[:, rows, :], sems.at[k])

    for k in range(SIDE + 1):
        piece(k).start()
    for near in range(SIDE):
        piece(near).wait()
        rows = pl.ds(near * SLOT_ROWS, SLOT_ROWS)
        total = got[0, rows, :].astype(jnp.float32)
        for far in range(1, SIDE):
            total = total + got[far, rows, :].astype(jnp.float32)
        out[near, pl.ds(0, SLOT_ROWS), :] = total
    piece(SIDE).wait()
    total = got[0, pl.ds(PART, SIDE * VEC_ROWS), :].astype(jnp.float32)
    for far in range(1, SIDE):
        total = total + got[far, pl.ds(PART, SIDE * VEC_ROWS), :].astype(jnp.float32)
    for near in range(SIDE):
        out[near, pl.ds(SLOT_ROWS, VEC_ROWS), :] = total[near * VEC_ROWS : (near + 1) * VEC_ROWS]
        out[near, pl.ds(SLOT_ROWS + VEC_ROWS, VEC_ROWS), :] = jnp.zeros((VEC_ROWS, LANES), jnp.float32)


def update_kernel(held, got, master, one, two, new_first, new_second, update_out, norms, vec_out):
    mine = held[lax.axis_index("dp")]
    for slot in range(CAP):
        rows = pl.ds(slot * ROWS, ROWS)
        gradient = got[0, rows, :]
        for k in range(1, SIDE):
            gradient = gradient + got[k, rows, :]
        weight = master[rows, :]
        first = beta_one * one[rows, :] + (1.0 - beta_one) * gradient
        second = beta_two * two[rows, :] + (1.0 - beta_two) * gradient * gradient
        update = first / fix_one / (jnp.sqrt(second / fix_two) + epsilon) + decay_rate * weight
        keep = mine > slot
        new_first[rows, :] = jnp.where(keep, first, 0.0)
        new_second[rows, :] = jnp.where(keep, second, 0.0)
        update_out[rows, :] = update
        weight_sq = jnp.sum((weight * weight).reshape(ROWS // 8, 8, LANES), axis=0)
        update_sq = jnp.sum((update * update).reshape(ROWS // 8, 8, LANES), axis=0)
        for k in range(SIDE):
            norms[k, pl.ds(2 * slot, 1), :] = jnp.sum(weight_sq, axis=0, keepdims=True)
            norms[k, pl.ds(2 * slot + 1, 1), :] = jnp.sum(update_sq, axis=0, keepdims=True)
    for k in range(SIDE):
        norms[k, pl.ds(2 * CAP, 8 - 2 * CAP), :] = jnp.zeros((8 - 2 * CAP, LANES), jnp.float32)
    rows = pl.ds(SLOT_ROWS, VEC_ROWS)
    total = got[0, rows, :]
    for k in range(1, SIDE):
        total = total + got[k, rows, :]
    vec_out[pl.ds(0, VEC_ROWS), :] = total
    vec_out[pl.ds(VEC_ROWS, VEC_ROWS), :] = total - total.astype(jnp.bfloat16).astype(jnp.float32)


def step_kernel(held, norms, master, update, vec, new_master, out):
    mine = held[lax.axis_index("dp")]
    total = norms[0]
    for k in range(1, SIDE):
        total = total + norms[k]
    total = jnp.sum(total, axis=1, keepdims=True)
    for slot in range(CAP):
        rows = pl.ds(slot * ROWS, ROWS)
        ratio = jnp.sqrt(total[2 * slot : 2 * slot + 1]) / jnp.sqrt(total[2 * slot + 1 : 2 * slot + 2])
        stepped = master[rows, :] - learn_rate * ratio * update[rows, :]
        stepped = jnp.where(mine > slot, stepped, 0.0)
        new_master[rows, :] = stepped
        rounded = stepped.astype(jnp.bfloat16)
        for k in range(SIDE):
            out[k, rows, :] = rounded
    rounded = vec[...].astype(jnp.bfloat16)
    for k in range(SIDE):
        out[k, pl.ds(SLOT_ROWS, 2 * VEC_ROWS), :] = rounded


def repeat_kernel(got, out):
    for near in range(SIDE):
        block = got[near]
        for k in range(SIDE):
            out[k, pl.ds(near * CHUNK, CHUNK), :] = block


def unpack_kernel(slots, got, vec_master, vec_first, vec_second, weights, new_master, new_first, new_second, staged, parts, results, in_sems, out_sems, part_sem, result_sems):
    count = slots.shape[0]
    batch = count // BATCHES
    by_z, by_y = strides(SIDE, 1)
    vec_rows_of = pltpu.make_async_copy(got.at[:, pl.ds(SLOT_ROWS, 2 * VEC_ROWS), :], parts, part_sem)
    vec_rows_of.start()

    for q in range(BATCHES):

        def fetch(m, _):
            slot = slots[m]
            z = lax.shift_right_logical(slot, 4)
            y = lax.shift_right_logical(slot, 1) & (SIDE - 1)
            row = pl.multiple_of((slot & 1) * ROWS, ROWS)
            source = got.at[z * by_z + y * by_y, pl.ds(row, ROWS), :]
            pltpu.make_async_copy(source, staged.at[m], in_sems.at[q]).start()
            return 0

        lax.fori_loop(q * batch, (q + 1) * batch, fetch, 0, unroll=7)

    vec_rows_of.wait()
    for far in range(SIDE):
        both = parts[pl.ds(far * SIDE, SIDE)].astype(jnp.float32)
        gradient = (both[:, :VEC_ROWS] + both[:, VEC_ROWS:]).reshape(SIDE * VEC_ROWS, LANES)
        first = beta_one * vec_first[far] + (1.0 - beta_one) * gradient
        second = beta_two * vec_second[far] + (1.0 - beta_two) * gradient * gradient
        results[1, far] = first
        results[2, far] = second
        results[0, far] = vec_master[far] - learn_rate * (first / fix_one) / (jnp.sqrt(second / fix_two) + epsilon)
    copies = [
        pltpu.make_async_copy(results.at[k], out, result_sems.at[k])
        for k, out in enumerate((new_master, new_first, new_second))
    ]
    for copy in copies:
        copy.start()
    for q in range(BATCHES):
        some = pl.ds(q * batch, batch)
        pltpu.make_async_copy(weights.at[some], staged.at[some], in_sems.at[q]).wait()
        copy = pltpu.make_async_copy(staged.at[some], weights.at[some], out_sems.at[q])
        copy.start()
        copies.append(copy)
    for copy in copies:
        copy.wait()


def to_rows(block):
    n, r, columns = block.shape
    return block.reshape(n, r, columns // LANES, LANES).transpose(0, 2, 1, 3).reshape(n, ROWS, LANES)


def from_rows(rows):
    n = rows.shape[0]
    return rows.reshape(n, ROWS // 2, 2, LANES).transpose(0, 2, 1, 3).reshape(n, 2, ROWS // 2 * LANES)


def vec_rows(block):
    return block.reshape(SIDE, SIDE, 4, LANES).transpose(0, 2, 1, 3).reshape(SIDE, 4 * SIDE, LANES)


def from_vec_rows(rows):
    return rows.reshape(SIDE, 4, SIDE, LANES).transpose(0, 2, 1, 3).reshape(SIDE * SIDE, 4 * LANES)


def axis_groups():
    def device(z, y, x, core):
        return (z * SIDE + y) * 8 + x * 2 + core

    side = range(SIDE)

    def along_y(core):
        return [[device(z, y, x, core) for y in side] for z in side for x in range(4)]

    def along_z(core):
        return [[device(z, y, x, core) for z in side] for y in side for x in range(4)]

    return along_y(0) + along_z(1), along_z(0) + along_y(1)


def exchange(x, groups):
    return lax.all_to_all(x, ("dp", "own"), 0, 0, axis_index_groups=groups, tiled=True)


def vmem(shape, dtype):
    return pltpu.VMEM(shape, dtype)


def close(x):
    return pltpu.with_memory_space_constraint(x, pltpu.VMEM)


def body(
    partial_grads,
    owner_group,
    master,
    moment_one,
    moment_two,
    vec_grads,
    vec_master,
    vec_first,
    vec_second,
):
    f32, bf16 = jnp.float32, jnp.bfloat16
    first_groups, second_groups = axis_groups()
    count = owner_group.shape[0]
    packed, slots, held = pl.pallas_call(
        pack_kernel,
        out_shape=(
            vmem((SIDE * WIDE, LANES), bf16),
            jax.ShapeDtypeStruct((count,), jnp.int32),
            jax.ShapeDtypeStruct((SIDE * SIDE,), jnp.int32),
        ),
        in_specs=[SMEM, ANY, ANY],
        out_specs=(VMEM, SMEM, SMEM),
        scratch_shapes=[pltpu.SemaphoreType.DMA],
        name="pack",
    )(owner_group, to_rows(partial_grads[0]), vec_rows(vec_grads[0]))
    got = exchange(packed.reshape(SIDE, WIDE, LANES), first_groups)
    partial = pl.pallas_call(
        partial_sum_kernel,
        out_shape=vmem((SIDE, CHUNK, LANES), f32),
        in_specs=[ANY],
        out_specs=VMEM,
        scratch_shapes=[pltpu.VMEM((SIDE, WIDE, LANES), bf16), pltpu.SemaphoreType.DMA((SIDE + 1,))],
        name="partial_sum",
    )(got)
    got = close(exchange(partial, second_groups))
    block = jax.ShapeDtypeStruct((SLOT_ROWS, LANES), f32)
    master_rows = close(to_rows(master).reshape(SLOT_ROWS, LANES))
    new_first, new_second, update, norms, vec_sum = pl.pallas_call(
        update_kernel,
        out_shape=(
            block,
            block,
            vmem((SLOT_ROWS, LANES), f32),
            vmem((SIDE, 8, LANES), f32),
            vmem((2 * VEC_ROWS, LANES), f32),
        ),
        in_specs=[SMEM] + [VMEM] * 4,
        out_specs=(VMEM,) * 5,
        name="update",
    )(
        held,
        got,
        master_rows,
        close(to_rows(moment_one).reshape(SLOT_ROWS, LANES)),
        close(to_rows(moment_two).reshape(SLOT_ROWS, LANES)),
    )
    norms = close(lax.all_to_all(norms, "own", 0, 0, tiled=True))
    new_master, out = pl.pallas_call(
        step_kernel,
        out_shape=(block, vmem((SIDE, CHUNK, LANES), bf16)),
        in_specs=[SMEM] + [VMEM] * 4,
        out_specs=(VMEM, VMEM),
        name="step",
    )(held, norms, master_rows, close(update), close(vec_sum))
    got = close(exchange(out, second_groups))
    out = pl.pallas_call(
        repeat_kernel,
        out_shape=vmem((SIDE, SIDE * CHUNK, LANES), bf16),
        in_specs=[VMEM],
        out_specs=VMEM,
        name="repeat",
    )(got)
    got = exchange(out, first_groups).reshape(SIDE * SIDE, CHUNK, LANES)
    vec_block = jax.ShapeDtypeStruct((SIDE, 4 * SIDE, LANES), f32)
    weights, new_vec_master, new_vec_first, new_vec_second = pl.pallas_call(
        unpack_kernel,
        out_shape=(jax.ShapeDtypeStruct((count, ROWS, LANES), bf16), vec_block, vec_block, vec_block),
        in_specs=[SMEM, ANY, VMEM, VMEM, VMEM],
        out_specs=(ANY, ANY, ANY, ANY),
        scratch_shapes=[
            pltpu.VMEM((count, ROWS, LANES), bf16),
            pltpu.VMEM((SIDE * SIDE, 2 * VEC_ROWS, LANES), bf16),
            pltpu.VMEM((3, SIDE, 4 * SIDE, LANES), f32),
            pltpu.SemaphoreType.DMA((BATCHES,)),
            pltpu.SemaphoreType.DMA((BATCHES,)),
            pltpu.SemaphoreType.DMA,
            pltpu.SemaphoreType.DMA((3,)),
        ],
        name="unpack",
    )(slots, got, *(close(vec_rows(x)) for x in (vec_master, vec_first, vec_second)))

    def blocks(rows):
        return from_rows(rows.reshape(CAP, ROWS, LANES))

    return (
        blocks(new_master),
        blocks(new_first),
        blocks(new_second),
        from_rows(weights),
        from_vec_rows(new_vec_master),
        from_vec_rows(new_vec_first),
        from_vec_rows(new_vec_second),
    )


def solution(mesh):
    placed = (
        P("dp", None, "own", None),
        P(),
        P("dp", "own", None),
        P("dp", "own", None),
        P("dp", "own", None),
        P("dp", None, "own"),
        P(None, "own"),
        P(None, "own"),
        P(None, "own"),
    )
    return jax.shard_map(
        body,
        mesh=mesh,
        in_specs=placed,
        out_specs=(
            P("dp", "own", None),
            P("dp", "own", None),
            P("dp", "own", None),
            P(None, "own", None),
            P(None, "own"),
            P(None, "own"),
            P(None, "own"),
        ),
        check_vma=False,
    )
```

```python
import functools

import jax
import jax.numpy as jnp
from jax import lax
from jax.experimental import pallas as pl
from jax.experimental.pallas import tpu as pltpu
from jax.sharding import PartitionSpec as P

beta_one = 0.9
beta_two = 0.95
fix_one = 1.0 - 0.9**10
fix_two = 1.0 - 0.95**10
epsilon = 1e-06
decay_rate = 0.1
learn_rate = 0.05

SIDE = 8
CAP = 2
LANES = 128
ROWS = 64
SLOT_ROWS = CAP * ROWS
VEC_ROWS = 4
PART = SIDE * SLOT_ROWS
WIDE = PART + SIDE * VEC_ROWS
CHUNK = SLOT_ROWS + 2 * VEC_ROWS
BATCHES = 4

VMEM = pl.BlockSpec(memory_space=pltpu.VMEM)
SMEM = pl.BlockSpec(memory_space=pltpu.SMEM)
ANY = pl.BlockSpec(memory_space=pl.ANY)


def strides(far, near):
    core = lax.rem(lax.axis_index("own"), 2)
    return jnp.where(core == 0, near, far), jnp.where(core == 0, far, near)


def row_of(slot, by_z, by_y, tile):
    z = lax.shift_right_logical(slot, 4)
    y = lax.shift_right_logical(slot, 1) & (SIDE - 1)
    return pl.multiple_of(z * by_z + y * by_y + (slot & 1) * ROWS, tile)


def pack_kernel(owner, grads, vecs, out, slots_out, mine, slots, held, sem, slots_sem):
    count = owner.shape[0]
    by_z, by_y = strides(WIDE, SLOT_ROWS)
    for far in range(SIDE):
        pltpu.make_async_copy(vecs.at[far], out.at[pl.ds(far * WIDE + PART, SIDE * VEC_ROWS), :], sem).start()

    def clear(g, _):
        held[g] = 0
        return 0

    lax.fori_loop(0, SIDE * SIDE, clear, 0, unroll=16)

    def send(m, _):
        g = owner[m]
        rank = held[g]
        held[g] = rank + 1
        slot = g * CAP + rank
        slots[m] = slot
        row = row_of(slot, by_z, by_y, 32)
        pltpu.make_async_copy(grads.at[m], out.at[pl.ds(row, ROWS), :], sem).start()
        return 0

    lax.fori_loop(0, count, send, 0, unroll=8)
    slots_copy = pltpu.make_async_copy(slots, slots_out, slots_sem)
    slots_copy.start()
    mine[...] = jnp.full(mine.shape, held[lax.axis_index("dp")], jnp.int32)

    def empty(g, _):
        filled = held[g]

        @pl.when(filled < CAP)
        def _():
            def put(slot):
                row = row_of(slot, by_z, by_y, 32)
                out[pl.ds(row, ROWS), :] = jnp.zeros((ROWS, LANES), out.dtype)

            put(g * CAP + 1)

            @pl.when(filled == 0)
            def _():
                put(g * CAP)

        return 0

    lax.fori_loop(0, SIDE * SIDE, empty, 0, unroll=4)
    filled_rows = out.at[pl.ds(0, count * ROWS + SIDE * SIDE * VEC_ROWS), :]
    pltpu.make_async_copy(filled_rows, filled_rows, sem).wait()
    slots_copy.wait()


def partial_sum_kernel(source, out, got, sems):
    def piece(k):
        rows = pl.ds(k * SLOT_ROWS, SLOT_ROWS if k < SIDE else SIDE * VEC_ROWS)
        return pltpu.make_async_copy(source.at[:, rows, :], got.at[:, rows, :], sems.at[k])

    for k in range(SIDE + 1):
        piece(k).start()
    for near in range(SIDE):
        piece(near).wait()
        rows = pl.ds(near * SLOT_ROWS, SLOT_ROWS)
        total = got[0, rows, :].astype(jnp.float32)
        for far in range(1, SIDE):
            total = total + got[far, rows, :].astype(jnp.float32)
        out[near, pl.ds(0, SLOT_ROWS), :] = total
    piece(SIDE).wait()
    total = got[0, pl.ds(PART, SIDE * VEC_ROWS), :].astype(jnp.float32)
    for far in range(1, SIDE):
        total = total + got[far, pl.ds(PART, SIDE * VEC_ROWS), :].astype(jnp.float32)
    for near in range(SIDE):
        out[near, pl.ds(SLOT_ROWS, VEC_ROWS), :] = total[near * VEC_ROWS : (near + 1) * VEC_ROWS]
        out[near, pl.ds(SLOT_ROWS + VEC_ROWS, VEC_ROWS), :] = jnp.zeros((VEC_ROWS, LANES), jnp.float32)


def update_kernel(mine, got, master, one, two, new_first, new_second, update_out, norms, vec_out):
    filled = mine[pl.ds(0, 1), :]
    for slot in range(CAP):
        rows = pl.ds(slot * ROWS, ROWS)
        gradient = got[0, rows, :]
        for k in range(1, SIDE):
            gradient = gradient + got[k, rows, :]
        weight = master[rows, :]
        first = beta_one * one[rows, :] + (1.0 - beta_one) * gradient
        second = beta_two * two[rows, :] + (1.0 - beta_two) * gradient * gradient
        update = first / fix_one / (jnp.sqrt(second / fix_two) + epsilon) + decay_rate * weight
        keep = filled > slot
        new_first[rows, :] = jnp.where(keep, first, 0.0)
        new_second[rows, :] = jnp.where(keep, second, 0.0)
        update_out[rows, :] = update
        weight_sq = jnp.sum((weight * weight).reshape(ROWS // 8, 8, LANES), axis=0)
        update_sq = jnp.sum((update * update).reshape(ROWS // 8, 8, LANES), axis=0)
        for k in range(SIDE):
            norms[k, pl.ds(2 * slot, 1), :] = jnp.sum(weight_sq, axis=0, keepdims=True)
            norms[k, pl.ds(2 * slot + 1, 1), :] = jnp.sum(update_sq, axis=0, keepdims=True)
    for k in range(SIDE):
        norms[k, pl.ds(2 * CAP, 8 - 2 * CAP), :] = jnp.zeros((8 - 2 * CAP, LANES), jnp.float32)
    rows = pl.ds(SLOT_ROWS, VEC_ROWS)
    total = got[0, rows, :]
    for k in range(1, SIDE):
        total = total + got[k, rows, :]
    vec_out[pl.ds(0, VEC_ROWS), :] = total
    vec_out[pl.ds(VEC_ROWS, VEC_ROWS), :] = total - total.astype(jnp.bfloat16).astype(jnp.float32)


def step_kernel(mine, norms, master, update, vec, new_master, out):
    filled = mine[pl.ds(0, 1), :]
    total = norms[0]
    for k in range(1, SIDE):
        total = total + norms[k]
    total = jnp.sum(total, axis=1, keepdims=True)
    for slot in range(CAP):
        rows = pl.ds(slot * ROWS, ROWS)
        ratio = jnp.sqrt(total[2 * slot : 2 * slot + 1]) / jnp.sqrt(total[2 * slot + 1 : 2 * slot + 2])
        stepped = master[rows, :] - learn_rate * ratio * update[rows, :]
        stepped = jnp.where(filled > slot, stepped, 0.0)
        new_master[rows, :] = stepped
        rounded = stepped.astype(jnp.bfloat16)
        for k in range(SIDE):
            out[k, rows, :] = rounded
    rounded = vec[...].astype(jnp.bfloat16)
    for k in range(SIDE):
        out[k, pl.ds(SLOT_ROWS, 2 * VEC_ROWS), :] = rounded


def repeat_kernel(got, out):
    for near in range(SIDE):
        block = got[near]
        for k in range(SIDE):
            out[k, pl.ds(near * CHUNK, CHUNK), :] = block


def unpack_kernel(
    slots, got, vec_master, vec_first, vec_second, *rest
):
    blocks_in, (weights, new_master, new_first, new_second), rest = rest[:3], rest[3:7], rest[7:]
    blocks_out, (staged, parts, results, in_sems, out_sems, part_sem, result_sems) = rest[:3], rest[3:]
    count = slots.shape[0]
    batch = count // BATCHES
    by_z, by_y = strides(SIDE, 1)
    vec_rows_of = pltpu.make_async_copy(got.at[:, pl.ds(SLOT_ROWS, 2 * VEC_ROWS), :], parts, part_sem)
    vec_rows_of.start()
    copies = [
        pltpu.make_async_copy(source, out, result_sems.at[3 + k])
        for k, (source, out) in enumerate(zip(blocks_in, blocks_out))
    ]
    for copy in copies:
        copy.start()

    for q in range(BATCHES):

        def fetch(m, _):
            slot = slots[m]
            z = lax.shift_right_logical(slot, 4)
            y = lax.shift_right_logical(slot, 1) & (SIDE - 1)
            row = pl.multiple_of((slot & 1) * ROWS, ROWS)
            source = got.at[z * by_z + y * by_y, pl.ds(row, ROWS), :]
            pltpu.make_async_copy(source, staged.at[m], in_sems.at[q]).start()
            return 0

        lax.fori_loop(q * batch, (q + 1) * batch, fetch, 0, unroll=7)

    vec_rows_of.wait()
    for far in range(SIDE):
        both = parts[pl.ds(far * SIDE, SIDE)].astype(jnp.float32)
        gradient = (both[:, :VEC_ROWS] + both[:, VEC_ROWS:]).reshape(SIDE * VEC_ROWS, LANES)
        first = beta_one * vec_first[far] + (1.0 - beta_one) * gradient
        second = beta_two * vec_second[far] + (1.0 - beta_two) * gradient * gradient
        results[1, far] = first
        results[2, far] = second
        results[0, far] = vec_master[far] - learn_rate * (first / fix_one) / (jnp.sqrt(second / fix_two) + epsilon)
    results_out = [
        pltpu.make_async_copy(results.at[k], out, result_sems.at[k])
        for k, out in enumerate((new_master, new_first, new_second))
    ]
    for copy in results_out:
        copy.start()
    copies += results_out
    for q in range(BATCHES):
        some = pl.ds(q * batch, batch)
        pltpu.make_async_copy(weights.at[some], staged.at[some], in_sems.at[q]).wait()
        copy = pltpu.make_async_copy(staged.at[some], weights.at[some], out_sems.at[q])
        copy.start()
        copies.append(copy)
    for copy in copies:
        copy.wait()


def to_rows(block):
    n, r, columns = block.shape
    return block.reshape(n, r, columns // LANES, LANES).transpose(0, 2, 1, 3).reshape(n, ROWS, LANES)


def from_rows(rows):
    n = rows.shape[0]
    return rows.reshape(n, ROWS // 2, 2, LANES).transpose(0, 2, 1, 3).reshape(n, 2, ROWS // 2 * LANES)


def vec_rows(block):
    return block.reshape(SIDE, SIDE, 4, LANES).transpose(0, 2, 1, 3).reshape(SIDE, 4 * SIDE, LANES)


def from_vec_rows(rows):
    return rows.reshape(SIDE, 4, SIDE, LANES).transpose(0, 2, 1, 3).reshape(SIDE * SIDE, 4 * LANES)


def axis_groups():
    def device(z, y, x, core):
        return (z * SIDE + y) * 8 + x * 2 + core

    side = range(SIDE)

    def along_y(core):
        return [[device(z, y, x, core) for y in side] for z in side for x in range(4)]

    def along_z(core):
        return [[device(z, y, x, core) for z in side] for y in side for x in range(4)]

    return along_y(0) + along_z(1), along_z(0) + along_y(1)


def exchange(x, groups):
    return lax.all_to_all(x, ("dp", "own"), 0, 0, axis_index_groups=groups, tiled=True)


def vmem(shape, dtype):
    return pltpu.VMEM(shape, dtype)


def close(x):
    return pltpu.with_memory_space_constraint(x, pltpu.VMEM)


def body(
    partial_grads,
    owner_group,
    master,
    moment_one,
    moment_two,
    vec_grads,
    vec_master,
    vec_first,
    vec_second,
):
    f32, bf16 = jnp.float32, jnp.bfloat16
    first_groups, second_groups = axis_groups()
    count = owner_group.shape[0]
    packed, slots, mine = pl.pallas_call(
        pack_kernel,
        out_shape=(
            vmem((SIDE * WIDE, LANES), bf16),
            jax.ShapeDtypeStruct((count,), jnp.int32),
            vmem((8, LANES), jnp.int32),
        ),
        in_specs=[SMEM, ANY, ANY],
        out_specs=(VMEM, ANY, VMEM),
        scratch_shapes=[
            pltpu.SMEM((count,), jnp.int32),
            pltpu.SMEM((SIDE * SIDE,), jnp.int32),
            pltpu.SemaphoreType.DMA,
            pltpu.SemaphoreType.DMA,
        ],
        name="pack",
    )(owner_group, to_rows(partial_grads[0]), vec_rows(vec_grads[0]))
    mine = close(mine)
    got = exchange(packed.reshape(SIDE, WIDE, LANES), first_groups)
    partial = pl.pallas_call(
        partial_sum_kernel,
        out_shape=vmem((SIDE, CHUNK, LANES), f32),
        in_specs=[ANY],
        out_specs=VMEM,
        scratch_shapes=[pltpu.VMEM((SIDE, WIDE, LANES), bf16), pltpu.SemaphoreType.DMA((SIDE + 1,))],
        name="partial_sum",
    )(got)
    got = close(exchange(partial, second_groups))
    block = vmem((SLOT_ROWS, LANES), f32)
    master_rows = close(to_rows(master).reshape(SLOT_ROWS, LANES))
    new_first, new_second, update, norms, vec_sum = pl.pallas_call(
        update_kernel,
        out_shape=(
            block,
            block,
            vmem((SLOT_ROWS, LANES), f32),
            vmem((SIDE, 8, LANES), f32),
            vmem((2 * VEC_ROWS, LANES), f32),
        ),
        in_specs=[VMEM] * 5,
        out_specs=(VMEM,) * 5,
        name="update",
    )(
        mine,
        got,
        master_rows,
        close(to_rows(moment_one).reshape(SLOT_ROWS, LANES)),
        close(to_rows(moment_two).reshape(SLOT_ROWS, LANES)),
    )
    norms = close(lax.all_to_all(norms, "own", 0, 0, tiled=True))
    new_master, out = pl.pallas_call(
        step_kernel,
        out_shape=(block, vmem((SIDE, CHUNK, LANES), bf16)),
        in_specs=[VMEM] * 5,
        out_specs=(VMEM, VMEM),
        name="step",
    )(mine, norms, master_rows, close(update), close(vec_sum))
    got = close(exchange(out, second_groups))
    out = pl.pallas_call(
        repeat_kernel,
        out_shape=vmem((SIDE, SIDE * CHUNK, LANES), bf16),
        in_specs=[VMEM],
        out_specs=VMEM,
        name="repeat",
    )(got)
    got = exchange(out, first_groups).reshape(SIDE * SIDE, CHUNK, LANES)
    vec_block = jax.ShapeDtypeStruct((SIDE, 4 * SIDE, LANES), f32)
    rows = jax.ShapeDtypeStruct((SLOT_ROWS, LANES), f32)
    weights, new_vec_master, new_vec_first, new_vec_second, new_master, new_first, new_second = pl.pallas_call(
        unpack_kernel,
        out_shape=(jax.ShapeDtypeStruct((count, ROWS, LANES), bf16), vec_block, vec_block, vec_block, rows, rows, rows),
        in_specs=[SMEM, ANY] + [VMEM] * 6,
        out_specs=(ANY,) * 7,
        scratch_shapes=[
            pltpu.VMEM((count, ROWS, LANES), bf16),
            pltpu.VMEM((SIDE * SIDE, 2 * VEC_ROWS, LANES), bf16),
            pltpu.VMEM((3, SIDE, 4 * SIDE, LANES), f32),
            pltpu.SemaphoreType.DMA((BATCHES,)),
            pltpu.SemaphoreType.DMA((BATCHES,)),
            pltpu.SemaphoreType.DMA,
            pltpu.SemaphoreType.DMA((6,)),
        ],
        name="unpack",
    )(
        slots,
        got,
        *(close(vec_rows(x)) for x in (vec_master, vec_first, vec_second)),
        *(close(x) for x in (new_master, new_first, new_second)),
    )

    def blocks(rows):
        return from_rows(rows.reshape(CAP, ROWS, LANES))

    return (
        blocks(new_master),
        blocks(new_first),
        blocks(new_second),
        from_rows(weights),
        from_vec_rows(new_vec_master),
        from_vec_rows(new_vec_first),
        from_vec_rows(new_vec_second),
    )


def solution(mesh):
    placed = (
        P("dp", None, "own", None),
        P(),
        P("dp", "own", None),
        P("dp", "own", None),
        P("dp", "own", None),
        P("dp", None, "own"),
        P(None, "own"),
        P(None, "own"),
        P(None, "own"),
    )
    return jax.shard_map(
        body,
        mesh=mesh,
        in_specs=placed,
        out_specs=(
            P("dp", "own", None),
            P("dp", "own", None),
            P("dp", "own", None),
            P(None, "own", None),
            P(None, "own"),
            P(None, "own"),
            P(None, "own"),
        ),
        check_vma=False,
    )
```

```python
import functools

import jax
import jax.numpy as jnp
from jax import lax
from jax.experimental import pallas as pl
from jax.experimental.pallas import tpu as pltpu
from jax.sharding import PartitionSpec as P

beta_one = 0.9
beta_two = 0.95
fix_one = 1.0 - 0.9**10
fix_two = 1.0 - 0.95**10
epsilon = 1e-06
decay_rate = 0.1
learn_rate = 0.05

SIDE = 8
CAP = 2
LANES = 128
ROWS = 64
SLOT_ROWS = CAP * ROWS
VEC_ROWS = 4
PART = SIDE * SLOT_ROWS
WIDE = PART + SIDE * VEC_ROWS
CHUNK = SLOT_ROWS + 2 * VEC_ROWS

VMEM = pl.BlockSpec(memory_space=pltpu.VMEM)
SMEM = pl.BlockSpec(memory_space=pltpu.SMEM)
ANY = pl.BlockSpec(memory_space=pl.ANY)


def strides(far, near):
    core = lax.rem(lax.axis_index("own"), 2)
    return jnp.where(core == 0, near, far), jnp.where(core == 0, far, near)


def row_of(slot, by_z, by_y, tile):
    z = lax.shift_right_logical(slot, 4)
    y = lax.shift_right_logical(slot, 1) & (SIDE - 1)
    return pl.multiple_of(z * by_z + y * by_y + (slot & 1) * ROWS, tile)


def pack_kernel(owner, grads, vecs, out, slots_out, mine, slots, held, sem, slots_sem):
    count = owner.shape[0]
    by_z, by_y = strides(WIDE, SLOT_ROWS)
    for far in range(SIDE):
        pltpu.make_async_copy(vecs.at[far], out.at[pl.ds(far * WIDE + PART, SIDE * VEC_ROWS), :], sem).start()

    def clear(g, _):
        held[g] = 0
        return 0

    lax.fori_loop(0, SIDE * SIDE, clear, 0, unroll=16)

    def send(m, _):
        g = owner[m]
        rank = held[g]
        held[g] = rank + 1
        slot = g * CAP + rank
        slots[m] = slot
        row = row_of(slot, by_z, by_y, 32)
        pltpu.make_async_copy(grads.at[m], out.at[pl.ds(row, ROWS), :], sem).start()
        return 0

    lax.fori_loop(0, count, send, 0, unroll=8)
    slots_copy = pltpu.make_async_copy(slots, slots_out, slots_sem)
    slots_copy.start()
    mine[...] = jnp.full(mine.shape, held[lax.axis_index("dp")], jnp.int32)

    filled_rows = out.at[pl.ds(0, count * ROWS + SIDE * SIDE * VEC_ROWS), :]
    pltpu.make_async_copy(filled_rows, filled_rows, sem).wait()
    slots_copy.wait()


def partial_sum_kernel(source, out, got, sems):
    def piece(k):
        rows = pl.ds(k * SLOT_ROWS, SLOT_ROWS if k < SIDE else SIDE * VEC_ROWS)
        return pltpu.make_async_copy(source.at[:, rows, :], got.at[:, rows, :], sems.at[k])

    for k in range(SIDE + 1):
        piece(k).start()
    for near in range(SIDE):
        piece(near).wait()
        rows = pl.ds(near * SLOT_ROWS, SLOT_ROWS)
        total = got[0, rows, :].astype(jnp.float32)
        for far in range(1, SIDE):
            total = total + got[far, rows, :].astype(jnp.float32)
        out[near, pl.ds(0, SLOT_ROWS), :] = total
    piece(SIDE).wait()
    total = got[0, pl.ds(PART, SIDE * VEC_ROWS), :].astype(jnp.float32)
    for far in range(1, SIDE):
        total = total + got[far, pl.ds(PART, SIDE * VEC_ROWS), :].astype(jnp.float32)
    for near in range(SIDE):
        out[near, pl.ds(SLOT_ROWS, VEC_ROWS), :] = total[near * VEC_ROWS : (near + 1) * VEC_ROWS]
        out[near, pl.ds(SLOT_ROWS + VEC_ROWS, VEC_ROWS), :] = jnp.zeros((VEC_ROWS, LANES), jnp.float32)


def update_kernel(mine, got, master, one, two, new_first, new_second, update_out, norms, vec_out):
    filled = mine[pl.ds(0, 1), :]
    for slot in range(CAP):
        rows = pl.ds(slot * ROWS, ROWS)
        gradient = got[0, rows, :]
        for k in range(1, SIDE):
            gradient = gradient + got[k, rows, :]
        keep = filled > slot
        gradient = jnp.where(keep, gradient, 0.0)
        weight = master[rows, :]
        first = beta_one * one[rows, :] + (1.0 - beta_one) * gradient
        second = beta_two * two[rows, :] + (1.0 - beta_two) * gradient * gradient
        update = first / fix_one / (jnp.sqrt(second / fix_two) + epsilon) + decay_rate * weight
        new_first[rows, :] = jnp.where(keep, first, 0.0)
        new_second[rows, :] = jnp.where(keep, second, 0.0)
        update_out[rows, :] = update
        weight_sq = jnp.sum((weight * weight).reshape(ROWS // 8, 8, LANES), axis=0)
        update_sq = jnp.sum((update * update).reshape(ROWS // 8, 8, LANES), axis=0)
        for k in range(SIDE):
            norms[k, pl.ds(2 * slot, 1), :] = jnp.sum(weight_sq, axis=0, keepdims=True)
            norms[k, pl.ds(2 * slot + 1, 1), :] = jnp.sum(update_sq, axis=0, keepdims=True)
    for k in range(SIDE):
        norms[k, pl.ds(2 * CAP, 8 - 2 * CAP), :] = jnp.zeros((8 - 2 * CAP, LANES), jnp.float32)
    rows = pl.ds(SLOT_ROWS, VEC_ROWS)
    total = got[0, rows, :]
    for k in range(1, SIDE):
        total = total + got[k, rows, :]
    vec_out[pl.ds(0, VEC_ROWS), :] = total
    vec_out[pl.ds(VEC_ROWS, VEC_ROWS), :] = total - total.astype(jnp.bfloat16).astype(jnp.float32)


def step_kernel(mine, norms, master, update, vec, new_master, out):
    filled = mine[pl.ds(0, 1), :]
    total = norms[0]
    for k in range(1, SIDE):
        total = total + norms[k]
    total = jnp.sum(total, axis=1, keepdims=True)
    for slot in range(CAP):
        rows = pl.ds(slot * ROWS, ROWS)
        ratio = jnp.sqrt(total[2 * slot : 2 * slot + 1]) / jnp.sqrt(total[2 * slot + 1 : 2 * slot + 2])
        stepped = master[rows, :] - learn_rate * ratio * update[rows, :]
        stepped = jnp.where(filled > slot, stepped, 0.0)
        new_master[rows, :] = stepped
        rounded = stepped.astype(jnp.bfloat16)
        for k in range(SIDE):
            out[k, rows, :] = rounded
    rounded = vec[...].astype(jnp.bfloat16)
    for k in range(SIDE):
        out[k, pl.ds(SLOT_ROWS, 2 * VEC_ROWS), :] = rounded


def repeat_kernel(got, out, sem):
    for k in range(SIDE):
        pltpu.make_async_copy(got, out.at[k], sem).start()
    pltpu.make_async_copy(out, out, sem).wait()


def unpack_kernel(slots, got, vec_master, vec_first, vec_second, *rest):
    blocks_in, (weights, new_master, new_first, new_second), rest = rest[:3], rest[3:7], rest[7:]
    blocks_out, (results, sem, result_sems) = rest[:3], rest[3:]
    count = slots.shape[0]
    by_z, by_y = strides(SIDE, 1)
    copies = [
        pltpu.make_async_copy(source, out, result_sems.at[3 + k])
        for k, (source, out) in enumerate(zip(blocks_in, blocks_out))
    ]
    for copy in copies:
        copy.start()

    def put(m, _):
        slot = slots[m]
        z = lax.shift_right_logical(slot, 4)
        y = lax.shift_right_logical(slot, 1) & (SIDE - 1)
        row = pl.multiple_of((slot & 1) * ROWS, ROWS)
        source = got.at[z * by_z + y * by_y, pl.ds(row, ROWS), :]
        pltpu.make_async_copy(source, weights.at[m], sem).start()
        return 0

    lax.fori_loop(0, count, put, 0, unroll=8)
    for far in range(SIDE):
        both = got[pl.ds(far * SIDE, SIDE), pl.ds(SLOT_ROWS, 2 * VEC_ROWS), :].astype(jnp.float32)
        gradient = (both[:, :VEC_ROWS] + both[:, VEC_ROWS:]).reshape(SIDE * VEC_ROWS, LANES)
        first = beta_one * vec_first[far] + (1.0 - beta_one) * gradient
        second = beta_two * vec_second[far] + (1.0 - beta_two) * gradient * gradient
        results[1, far] = first
        results[2, far] = second
        results[0, far] = vec_master[far] - learn_rate * (first / fix_one) / (jnp.sqrt(second / fix_two) + epsilon)
    for k, out in enumerate((new_master, new_first, new_second)):
        copies.append(pltpu.make_async_copy(results.at[k], out, result_sems.at[k]))
        copies[-1].start()
    pltpu.make_async_copy(weights, weights, sem).wait()
    for copy in copies:
        copy.wait()


def to_rows(block):
    n, r, columns = block.shape
    return block.reshape(n, r, columns // LANES, LANES).transpose(0, 2, 1, 3).reshape(n, ROWS, LANES)


def from_rows(rows):
    n = rows.shape[0]
    return rows.reshape(n, ROWS // 2, 2, LANES).transpose(0, 2, 1, 3).reshape(n, 2, ROWS // 2 * LANES)


def vec_rows(block):
    return block.reshape(SIDE, SIDE, 4, LANES).transpose(0, 2, 1, 3).reshape(SIDE, 4 * SIDE, LANES)


def from_vec_rows(rows):
    return rows.reshape(SIDE, 4, SIDE, LANES).transpose(0, 2, 1, 3).reshape(SIDE * SIDE, 4 * LANES)


def axis_groups():
    def device(z, y, x, core):
        return (z * SIDE + y) * 8 + x * 2 + core

    side = range(SIDE)

    def along_y(core):
        return [[device(z, y, x, core) for y in side] for z in side for x in range(4)]

    def along_z(core):
        return [[device(z, y, x, core) for z in side] for y in side for x in range(4)]

    return along_y(0) + along_z(1), along_z(0) + along_y(1)


def exchange(x, groups):
    return lax.all_to_all(x, ("dp", "own"), 0, 0, axis_index_groups=groups, tiled=True)


def vmem(shape, dtype):
    return pltpu.VMEM(shape, dtype)


def close(x):
    return pltpu.with_memory_space_constraint(x, pltpu.VMEM)


def body(
    partial_grads,
    owner_group,
    master,
    moment_one,
    moment_two,
    vec_grads,
    vec_master,
    vec_first,
    vec_second,
):
    f32, bf16 = jnp.float32, jnp.bfloat16
    first_groups, second_groups = axis_groups()
    count = owner_group.shape[0]
    packed, slots, mine = pl.pallas_call(
        pack_kernel,
        out_shape=(
            vmem((SIDE * WIDE, LANES), bf16),
            jax.ShapeDtypeStruct((count,), jnp.int32),
            vmem((8, LANES), jnp.int32),
        ),
        in_specs=[SMEM, ANY, ANY],
        out_specs=(VMEM, ANY, VMEM),
        scratch_shapes=[
            pltpu.SMEM((count,), jnp.int32),
            pltpu.SMEM((SIDE * SIDE,), jnp.int32),
            pltpu.SemaphoreType.DMA,
            pltpu.SemaphoreType.DMA,
        ],
        name="pack",
    )(owner_group, to_rows(partial_grads[0]), vec_rows(vec_grads[0]))
    mine = close(mine)
    got = exchange(packed.reshape(SIDE, WIDE, LANES), first_groups)
    partial = pl.pallas_call(
        partial_sum_kernel,
        out_shape=vmem((SIDE, CHUNK, LANES), f32),
        in_specs=[ANY],
        out_specs=VMEM,
        scratch_shapes=[pltpu.VMEM((SIDE, WIDE, LANES), bf16), pltpu.SemaphoreType.DMA((SIDE + 1,))],
        name="partial_sum",
    )(got)
    got = close(exchange(partial, second_groups))
    block = vmem((SLOT_ROWS, LANES), f32)
    master_rows = close(to_rows(master).reshape(SLOT_ROWS, LANES))
    new_first, new_second, update, norms, vec_sum = pl.pallas_call(
        update_kernel,
        out_shape=(
            block,
            block,
            vmem((SLOT_ROWS, LANES), f32),
            vmem((SIDE, 8, LANES), f32),
            vmem((2 * VEC_ROWS, LANES), f32),
        ),
        in_specs=[VMEM] * 5,
        out_specs=(VMEM,) * 5,
        name="update",
    )(
        mine,
        got,
        master_rows,
        close(to_rows(moment_one).reshape(SLOT_ROWS, LANES)),
        close(to_rows(moment_two).reshape(SLOT_ROWS, LANES)),
    )
    norms = close(lax.all_to_all(norms, "own", 0, 0, tiled=True))
    new_master, out = pl.pallas_call(
        step_kernel,
        out_shape=(block, vmem((SIDE, CHUNK, LANES), bf16)),
        in_specs=[VMEM] * 5,
        out_specs=(VMEM, VMEM),
        name="step",
    )(mine, norms, master_rows, close(update), close(vec_sum))
    got = close(exchange(out, second_groups).reshape(SIDE * CHUNK, LANES))
    out = pl.pallas_call(
        repeat_kernel,
        out_shape=jax.ShapeDtypeStruct((SIDE, SIDE * CHUNK, LANES), bf16),
        in_specs=[VMEM],
        out_specs=ANY,
        scratch_shapes=[pltpu.SemaphoreType.DMA],
        name="repeat",
    )(got)
    got = close(exchange(out, first_groups).reshape(SIDE * SIDE, CHUNK, LANES))
    vec_block = jax.ShapeDtypeStruct((SIDE, 4 * SIDE, LANES), f32)
    rows = jax.ShapeDtypeStruct((SLOT_ROWS, LANES), f32)
    weights, new_vec_master, new_vec_first, new_vec_second, new_master, new_first, new_second = pl.pallas_call(
        unpack_kernel,
        out_shape=(jax.ShapeDtypeStruct((count, ROWS, LANES), bf16), vec_block, vec_block, vec_block, rows, rows, rows),
        in_specs=[SMEM] + [VMEM] * 7,
        out_specs=(ANY,) * 7,
        scratch_shapes=[
            pltpu.VMEM((3, SIDE, 4 * SIDE, LANES), f32),
            pltpu.SemaphoreType.DMA,
            pltpu.SemaphoreType.DMA((6,)),
        ],
        name="unpack",
    )(
        slots,
        got,
        *(close(vec_rows(x)) for x in (vec_master, vec_first, vec_second)),
        *(close(x) for x in (new_master, new_first, new_second)),
    )

    def blocks(rows):
        return from_rows(rows.reshape(CAP, ROWS, LANES))

    return (
        blocks(new_master),
        blocks(new_first),
        blocks(new_second),
        from_rows(weights),
        from_vec_rows(new_vec_master),
        from_vec_rows(new_vec_first),
        from_vec_rows(new_vec_second),
    )


def solution(mesh):
    placed = (
        P("dp", None, "own", None),
        P(),
        P("dp", "own", None),
        P("dp", "own", None),
        P("dp", "own", None),
        P("dp", None, "own"),
        P(None, "own"),
        P(None, "own"),
        P(None, "own"),
    )
    return jax.shard_map(
        body,
        mesh=mesh,
        in_specs=placed,
        out_specs=(
            P("dp", "own", None),
            P("dp", "own", None),
            P("dp", "own", None),
            P(None, "own", None),
            P(None, "own"),
            P(None, "own"),
            P(None, "own"),
        ),
        check_vma=False,
    )
```
